32 devices in a mesh: groups: 2 (over y), res: 4 (over z), col: 2 (over x), seq: 2 (over core).
Axes of the slice: x: 2, y: 2, z: 4, core: 2. Of those that a mesh axis runs over, the one named last changes fastest.
Arguments:
- alignment_states: bfloat16 [128, 128, 256], P(('groups', 'res', 'seq'), 'col'), parts along dimension 0, may hold values from -6 to 6
- standardize_scale: float32 [256], replicated, may hold values from 0.5 to 1.5
- standardize_shift: float32 [256], replicated, may hold values from -3 to 3
- first_factor_coeffs: bfloat16 [256, 32], replicated, may hold values from -0.375 to 0.375
- first_factor_offset: float32 [32], replicated, may hold values from -3 to 3
- second_factor_coeffs: bfloat16 [256, 32], replicated, may hold values from -0.375 to 0.375
- second_factor_offset: float32 [32], replicated, may hold values from -3 to 3
- final_coeffs: bfloat16 [1024, 128], replicated, may hold values from -0.1875 to 0.1875
- final_offset: float32 [128], replicated, may hold values from -3 to 3
Outputs:
- pair: bfloat16 [4, 64, 128, 128], P('groups', ('res', 'seq'), 'col'), parts along dimension 0
The draws below stay inside these ranges and needn't reach their ends.
There are 2 independent parts, one for each index of `groups`. The reference program is written for one: setup_inputs(seed, part) draws one part's arguments, and reference() takes and returns one part's arrays. A program takes and returns all parts, laid end to end along the dimension named above; an argument that names none is the same for every part. Nothing has to cross between parts.
All inputs are finite; a program needn't handle non-finite values.
Results may differ from the reference program's by a relative error of at most 0.0037.
Values may be sent and summed in bfloat16 or wider, within the bound.
A program may use at most 64 MiB of HBM per device.

```python
import jax
import jax.numpy as jnp
from jax import lax

ALIGN_DIM = 256
HIDDEN_DIM = 32
P_SIZE = 128
RES_DEV = 16
SEQ_DEV = 8
RSPAN = 64
NUM_POSITIONS = 128
NUM_ALIGNED = 64
N_RES = 4
N_COL = 2
N_SEQ = 2


def shard_levels(key, extent, shards, least, top_value):
    level, own = 1.0, jax.random.fold_in(key, 6)
    for axis_at, shards_of in shards:
        draws = jnp.exp(jax.random.uniform(jax.random.fold_in(own, axis_at), (shards_of,), jnp.float32, least / len(shards), top_value / len(shards)))
        level = level * jnp.repeat(draws, extent[axis_at] // shards_of).reshape([-1 if axis == axis_at else 1 for axis in range(len(extent))])
    return level


def gaussian(rng, extent, width, bound, cuts=(), dtype=jnp.bfloat16):
    array = width * jax.random.normal(rng, extent, jnp.float32)
    if cuts:
        array = array * shard_levels(rng, extent, cuts, -0.22, 0.18)
    return jnp.clip(array, -bound, bound).astype(dtype)


def setup_inputs(seed: int = 0, part: int = 0) -> dict:
    splits = jax.random.split(jax.random.key(seed), 10)
    own_keys = jax.random.split(jax.random.fold_in(splits[9], part), 10)
    alignment_states = gaussian(own_keys[0], (NUM_ALIGNED, NUM_POSITIONS, ALIGN_DIM), 1.0, 6.0, ((0, 8), (1, 2)))
    standardize_scale = jnp.clip(1.0 + 0.1 * jax.random.normal(splits[1], (ALIGN_DIM,), jnp.float32), 0.5, 1.5)
    standardize_shift = gaussian(splits[2], (ALIGN_DIM,), 0.5, 3.0, (), jnp.float32)
    first_factor_coeffs = gaussian(splits[3], (ALIGN_DIM, HIDDEN_DIM), ALIGN_DIM ** -0.5, 0.375)
    first_factor_offset = gaussian(splits[4], (HIDDEN_DIM,), 0.5, 3.0, (), jnp.float32)
    second_factor_coeffs = gaussian(splits[5], (ALIGN_DIM, HIDDEN_DIM), ALIGN_DIM ** -0.5, 0.375)
    second_factor_offset = gaussian(splits[6], (HIDDEN_DIM,), 0.5, 3.0, (), jnp.float32)
    final_coeffs = gaussian(splits[7], (HIDDEN_DIM * HIDDEN_DIM, P_SIZE), (HIDDEN_DIM * HIDDEN_DIM) ** -0.5, 0.1875)
    final_offset = gaussian(splits[8], (P_SIZE,), 0.5, 3.0, (), jnp.float32)
    return {"alignment_states": alignment_states, "standardize_scale": standardize_scale, "standardize_shift": standardize_shift, "first_factor_coeffs": first_factor_coeffs, "first_factor_offset": first_factor_offset, "second_factor_coeffs": second_factor_coeffs, "second_factor_offset": second_factor_offset, "final_coeffs": final_coeffs, "final_offset": final_offset}


def affine_map_apply(alignment_states, standardize_scale, standardize_shift, coefficient_table, offset_terms):
    input_tensor = alignment_states.astype(jnp.float32)
    mean = lax.optimization_barrier(jnp.mean(input_tensor, axis=-1, keepdims=True))
    centred = input_tensor - mean
    variance = lax.optimization_barrier(jnp.mean(centred * centred, axis=-1, keepdims=True))
    normed = (centred * lax.rsqrt(variance + 1e-05) * standardize_scale + standardize_shift).astype(jnp.bfloat16)
    normed = lax.optimization_barrier(normed)
    out = jnp.einsum('src,ck->srk', normed.astype(jnp.float32), coefficient_table.astype(jnp.float32)) + offset_terms
    return out.astype(jnp.bfloat16)

def reference(alignment_states, standardize_scale, standardize_shift, first_factor_coeffs, first_factor_offset, second_factor_coeffs, second_factor_offset, final_coeffs, final_offset):
    first_factor_states = affine_map_apply(alignment_states, standardize_scale, standardize_shift, first_factor_coeffs, first_factor_offset)
    second_factor_states = affine_map_apply(alignment_states, standardize_scale, standardize_shift, second_factor_coeffs, second_factor_offset)
    left_five = first_factor_states.astype(jnp.float32).reshape(N_RES, N_SEQ, SEQ_DEV, NUM_POSITIONS, HIDDEN_DIM)
    right_f = second_factor_states.astype(jnp.float32)
    w_flat = final_coeffs.astype(jnp.float32)

    def column_block(start):
        block = lax.dynamic_slice_in_dim(right_f, start, RES_DEV, 1)
        block = block.reshape(N_RES, N_SEQ, SEQ_DEV, RES_DEV, HIDDEN_DIM)
        outer = jnp.einsum('agtic,agtje->gijce', left_five, block).astype(jnp.bfloat16)
        outer = lax.optimization_barrier(outer).astype(jnp.float32)
        outer = outer.reshape(N_SEQ, NUM_POSITIONS, RES_DEV, HIDDEN_DIM * HIDDEN_DIM)
        summed = jnp.einsum('gijk,kp->ijp', outer, w_flat)
        return (summed / NUM_ALIGNED + final_offset).astype(jnp.bfloat16)
    starts = (jnp.arange(NUM_POSITIONS // RES_DEV) * RES_DEV).astype(jnp.int32)
    blocks = lax.map(column_block, starts)
    pair = blocks.transpose(1, 0, 2, 3).reshape(NUM_POSITIONS, NUM_POSITIONS, P_SIZE)
    return pair.reshape(N_COL, RSPAN, NUM_POSITIONS, P_SIZE)
```

```python
import functools

import jax
import jax.numpy as jnp
from jax import lax
from jax.experimental import pallas as pl
from jax.experimental.pallas import tpu as pltpu
from jax.sharding import PartitionSpec as P

MESH = pl.DeviceIdType.MESH
F32 = jnp.float32
BF16 = jnp.bfloat16


def one_hot(shape, wanted):
    row = lax.broadcasted_iota(jnp.int32, shape, 0)
    col = lax.broadcasted_iota(jnp.int32, shape, 1)
    return jnp.where(wanted(row, col), 1.0, 0.0)


def column_of(row, size):
    spread = jnp.broadcast_to(row, (size, size))
    return jnp.sum(one_hot((size, size), lambda r, c: r == c) * spread, axis=1, keepdims=True)


def matmul(a, b):
    return jnp.dot(a, b, preferred_element_type=F32)


def kernel(
    dims,
    msa,
    scale,
    shift,
    w_left,
    b_left,
    w_right,
    b_right,
    w_hbm,
    b_out,
    out,
    w_vmem,
    w_f32,
    w_flip,
    both_s,
    turn_s,
    left_send,
    left_all,
    left_flip,
    right_all,
    outer,
    w_sem,
    left_ssem,
    left_rsem,
    right_ssem,
    right_rsem,
):
    n_res, n_col, n_seq, seqs, span, width, chans, pairs = dims
    n_src = n_res * n_seq
    n_all = n_src * n_col
    fold = max(1, 128 // span)
    high = chans // fold
    rows = span // n_src
    lanes = fold * span
    group = outer.shape[2] // lanes
    res, col, seq = lax.axis_index("res"), lax.axis_index("col"), lax.axis_index("seq")
    src = res * n_seq + seq
    me = col * n_src + src

    def place(index):
        at = lax.rem(index, n_src)
        return {"res": at // n_seq, "col": index // n_src, "seq": lax.rem(at, n_seq)}

    def each(count, body):
        if count <= 16:
            for step in range(1, count):
                body(step)
        else:
            lax.fori_loop(1, count, lambda step, _: (body(step), 0)[1], 0)

    barrier = pltpu.get_barrier_semaphore()

    def greet(step):
        pl.semaphore_signal(barrier, inc=1, device_id=place(lax.rem(me + step, n_all)), device_id_type=MESH)

    each(n_all, greet)
    w_copy = pltpu.make_async_copy(w_hbm, w_vmem, w_sem)
    w_copy.start()

    w_both = jnp.concatenate([w_left[...], w_right[...]], axis=1)
    b_both = jnp.concatenate([b_left[...], b_right[...]], axis=1)
    for s in range(seqs):
        x = msa[s].astype(F32)
        mean = jnp.mean(x, axis=-1, keepdims=True)
        centred = x - mean
        variance = jnp.mean(centred * centred, axis=-1, keepdims=True)
        normed = (centred * lax.rsqrt(variance + 1e-05) * scale[...] + shift[...]).astype(BF16)
        both = matmul(normed, w_both) + b_both
        both_s[pl.ds(s * span, span), :] = both
        pick = one_hot(
            (chans, 2 * chans), lambda r, c: c == chans + lax.rem(r, high) * fold + r // high
        ).astype(BF16)
        turned = lax.dot_general(
            pick, both.astype(BF16), (((1,), (1,)), ((), ())), preferred_element_type=F32
        )
        parts = [turned[k * high : (k + 1) * high] for k in range(fold)]
        whole = parts[0] if fold == 1 else jnp.concatenate(parts, axis=1)
        for k in range(lanes // 128):
            turn_s[k, pl.ds(s * high, high), :] = whole[:, k * 128 : (k + 1) * 128]

    for e in range(high):
        for k in range(lanes // 128):
            right_all[src, e, :, pl.ds(k * 128, 128)] = turn_s[
                k, pl.ds(e, seqs, stride=high), :
            ].astype(BF16)

    total = None
    for v in range(rows):
        got = jnp.concatenate(
            [both_s[pl.ds(b * rows + v, seqs, stride=span), :] for b in range(n_src)], axis=0
        )
        spot = one_hot(
            (2 * chans, rows * chans), lambda r, c: (c == v * chans + r) & (r < chans)
        ).astype(BF16)
        term = matmul(got.astype(BF16), spot)
        total = term if total is None else total + term
    total = total.reshape(n_src, seqs, rows * chans).astype(BF16)
    left_send[...] = total

    pl.semaphore_wait(barrier, n_all - 1)

    def left_copy(step):
        to = lax.rem(me + step, n_all)
        return pltpu.make_async_remote_copy(
            src_ref=left_send.at[lax.rem(to, n_src)],
            dst_ref=left_all.at[me],
            send_sem=left_ssem.at[step],
            recv_sem=left_rsem.at[step],
            device_id=place(to),
            device_id_type=MESH,
        )

    def right_copy(step):
        to = lax.rem(src + step, n_src)
        return pltpu.make_async_remote_copy(
            src_ref=right_all.at[src],
            dst_ref=right_all.at[src],
            send_sem=right_ssem.at[step],
            recv_sem=right_rsem.at[step],
            device_id=place(col * n_src + to),
            device_id_type=MESH,
        )

    each(n_all, lambda step: left_copy(step).start())
    each(n_src, lambda step: right_copy(step).start())
    left_all[me] = left_send[src]

    w_copy.wait()
    w_f32[...] = w_vmem[...].astype(F32)
    chunk = 4
    for at in range(0, chans, chunk):
        taken = jnp.concatenate(
            [w_f32[pl.ds(e, chans, stride=chans), :] for e in range(at, at + chunk)], axis=0
        )
        w_flip[:, pl.ds(at * chans, chunk * chans)] = taken.T.astype(BF16)
    offset = column_of(b_out[...], pairs)

    each(n_all, lambda step: left_copy(step).wait())
    deep = fold * n_src * seqs
    for u in range(n_col // fold):
        taken = left_all[pl.ds(u * fold * n_src, fold * n_src)].astype(F32)
        left_flip[u] = taken.reshape(deep, rows * chans).T.astype(BF16)
    each(n_src, lambda step: right_copy(step).wait())

    factor = 1.0 / float(seqs * n_src)
    for u in range(n_col // fold):
        left = left_flip[u]
        for h in range(high):
            block = right_all[:, h].astype(F32).reshape(n_src * seqs, lanes)
            if fold == 1:
                wide = block
            else:
                lane = lax.broadcasted_iota(jnp.int32, block.shape, 1) // span
                columns = []
                for k in range(fold):
                    tall = []
                    for t in range(fold):
                        moved = block if t == k else pltpu.roll(block, ((t - k) % fold) * span, 1)
                        tall.append(jnp.where(lane == t, moved, 0.0))
                    columns.append(jnp.concatenate(tall, axis=0))
                wide = jnp.concatenate(columns, axis=1)
            product = matmul(left, wide.astype(BF16)).astype(BF16)
            for k in range(fold):
                for v in range(rows):
                    outer[
                        v // group,
                        pl.ds((h * fold + k) * chans, chans),
                        pl.ds((v % group) * lanes, lanes),
                    ] = product[v * chans : (v + 1) * chans, k * lanes : (k + 1) * lanes]
        for g in range(rows // group):
            summed = matmul(w_flip[...], outer[g])
            done = (summed * factor + offset).astype(BF16).T
            for k in range(group):
                for t in range(fold):
                    out[u * fold + t, g * group + k] = done[
                        k * lanes + t * span : k * lanes + (t + 1) * span
                    ]


def per_device(msa, scale, shift, w_left, b_left, w_right, b_right, w_out, b_out):
    seqs, span, width = msa.shape
    n_res, n_col, n_seq = lax.axis_size("res"), lax.axis_size("col"), lax.axis_size("seq")
    chans = w_left.shape[1]
    pairs = w_out.shape[1]
    n_src = n_res * n_seq
    fold = max(1, 128 // span)
    high = chans // fold
    rows = span // n_src
    lanes = fold * span
    group = max(1, 256 // lanes)
    deep = fold * n_src * seqs
    dims = (n_res, n_col, n_seq, seqs, span, width, chans, pairs)
    vmem = pl.BlockSpec(memory_space=pltpu.VMEM)
    return pl.pallas_call(
        functools.partial(kernel, dims),
        out_shape=jax.ShapeDtypeStruct((n_col, rows, span, pairs), BF16),
        in_specs=[vmem] * 7 + [pl.BlockSpec(memory_space=pl.ANY), vmem],
        out_specs=vmem,
        scratch_shapes=[
            pltpu.VMEM(w_out.shape, BF16),
            pltpu.VMEM(w_out.shape, F32),
            pltpu.VMEM((pairs, chans * chans), BF16),
            pltpu.VMEM((seqs * span, 2 * chans), F32),
            pltpu.VMEM((lanes // 128, seqs * high, 128), F32),
            pltpu.VMEM((n_src, seqs, rows * chans), BF16),
            pltpu.VMEM((n_src * n_col, seqs, rows * chans), BF16),
            pltpu.VMEM((n_col // fold, rows * chans, deep), BF16),
            pltpu.VMEM((n_src, high, seqs, lanes), BF16),
            pltpu.VMEM((rows // group, chans * chans, group * lanes), BF16),
            pltpu.SemaphoreType.DMA,
            pltpu.SemaphoreType.DMA((n_src * n_col,)),
            pltpu.SemaphoreType.DMA((n_src * n_col,)),
            pltpu.SemaphoreType.DMA((n_src,)),
            pltpu.SemaphoreType.DMA((n_src,)),
        ],
        compiler_params=pltpu.CompilerParams(collective_id=0, has_side_effects=True),
    )(
        msa,
        scale.reshape(1, width),
        shift.reshape(1, width),
        w_left,
        b_left.reshape(1, chans),
        w_right,
        b_right.reshape(1, chans),
        w_out,
        b_out.reshape(1, pairs),
    )


def solution(mesh):
    return jax.shard_map(
        per_device,
        mesh=mesh,
        in_specs=(P(("groups", "res", "seq"), "col", None), P(), P(), P(), P(), P(), P(), P(), P()),
        out_specs=P("groups", ("res", "seq"), "col", None),
        check_vma=False,
    )
```

```python
import functools

import jax
import jax.numpy as jnp
from jax import lax
from jax.experimental import pallas as pl
from jax.experimental.pallas import tpu as pltpu
from jax.sharding import PartitionSpec as P

MESH = pl.DeviceIdType.MESH
F32 = jnp.float32
BF16 = jnp.bfloat16


def one_hot(shape, wanted):
    row = lax.broadcasted_iota(jnp.int32, shape, 0)
    col = lax.broadcasted_iota(jnp.int32, shape, 1)
    return jnp.where(wanted(row, col), 1.0, 0.0)


def column_of(row, size):
    spread = jnp.broadcast_to(row, (size, size))
    return jnp.sum(one_hot((size, size), lambda r, c: r == c) * spread, axis=1, keepdims=True)


def matmul(a, b):
    return jnp.dot(a, b, preferred_element_type=F32)


def matmul_turned(a, b):
    return lax.dot_general(a, b, (((1,), (1,)), ((), ())), preferred_element_type=F32)


def kernel(
    dims,
    msa,
    scale,
    shift,
    w_left,
    b_left,
    w_right,
    b_right,
    w_hbm,
    b_out,
    out,
    w_vmem,
    w_f32,
    w_flip,
    both_s,
    turn_s,
    left_send,
    left_all,
    left_flip,
    right_all,
    outer,
    w_sem,
    left_ssem,
    left_rsem,
    right_ssem,
    right_rsem,
):
    n_res, n_col, n_seq, seqs, span, width, chans, pairs = dims
    n_src = n_res * n_seq
    n_all = n_src * n_col
    fold = max(1, 128 // span)
    high = chans // fold
    rows = span // n_src
    lanes = fold * span
    group = outer.shape[2] // lanes
    res, col, seq = lax.axis_index("res"), lax.axis_index("col"), lax.axis_index("seq")
    src = res * n_seq + seq
    me = col * n_src + src

    def place(index):
        at = lax.rem(index, n_src)
        return {"res": at // n_seq, "col": index // n_src, "seq": lax.rem(at, n_seq)}

    def each(count, body):
        if count <= 16:
            for step in range(1, count):
                body(step)
        else:
            lax.fori_loop(1, count, lambda step, _: (body(step), 0)[1], 0)

    barrier = pltpu.get_barrier_semaphore()

    def greet(step):
        pl.semaphore_signal(barrier, inc=1, device_id=place(lax.rem(me + step, n_all)), device_id_type=MESH)

    each(n_all, greet)
    w_copy = pltpu.make_async_copy(w_hbm, w_vmem, w_sem)
    w_copy.start()

    w_both = jnp.concatenate([w_left[...], w_right[...]], axis=0)
    b_both = jnp.concatenate([b_left[...], b_right[...]], axis=1)
    for s in range(seqs):
        x = msa[s].astype(F32)
        mean = jnp.mean(x, axis=-1, keepdims=True)
        centred = x - mean
        variance = jnp.mean(centred * centred, axis=-1, keepdims=True)
        normed = (centred * lax.rsqrt(variance + 1e-05) * scale[...] + shift[...]).astype(BF16)
        both = matmul_turned(normed, w_both) + b_both
        both_s[pl.ds(s * span, span), :] = both
        pick = one_hot(
            (chans, 2 * chans), lambda r, c: c == chans + lax.rem(r, high) * fold + r // high
        ).astype(BF16)
        turned = matmul_turned(pick, both.astype(BF16))
        parts = [turned[k * high : (k + 1) * high] for k in range(fold)]
        whole = parts[0] if fold == 1 else jnp.concatenate(parts, axis=1)
        for k in range(lanes // 128):
            turn_s[k, pl.ds(s * high, high), :] = whole[:, k * 128 : (k + 1) * 128]

    for e in range(high):
        for k in range(lanes // 128):
            right_all[src, e, :, pl.ds(k * 128, 128)] = turn_s[
                k, pl.ds(e, seqs, stride=high), :
            ].astype(BF16)

    total = None
    for v in range(rows):
        got = jnp.concatenate(
            [both_s[pl.ds(b * rows + v, seqs, stride=span), :] for b in range(n_src)], axis=0
        )
        spot = one_hot(
            (2 * chans, rows * chans), lambda r, c: (c == v * chans + r) & (r < chans)
        ).astype(BF16)
        term = matmul(got.astype(BF16), spot)
        total = term if total is None else total + term
    total = total.reshape(n_src, seqs, rows * chans).astype(BF16)
    left_send[...] = total

    pl.semaphore_wait(barrier, n_all - 1)

    def left_copy(step):
        to = lax.rem(me + step, n_all)
        return pltpu.make_async_remote_copy(
            src_ref=left_send.at[lax.rem(to, n_src)],
            dst_ref=left_all.at[me],
            send_sem=left_ssem.at[step],
            recv_sem=left_rsem.at[step],
            device_id=place(to),
            device_id_type=MESH,
        )

    def right_copy(step):
        to = lax.rem(src + step, n_src)
        return pltpu.make_async_remote_copy(
            src_ref=right_all.at[src],
            dst_ref=right_all.at[src],
            send_sem=right_ssem.at[step],
            recv_sem=right_rsem.at[step],
            device_id=place(col * n_src + to),
            device_id_type=MESH,
        )

    each(n_all, lambda step: left_copy(step).start())
    each(n_src, lambda step: right_copy(step).start())
    left_all[me] = left_send[src]

    w_copy.wait()
    w_f32[...] = w_vmem[...].astype(F32)
    chunk = 4
    for at in range(0, chans, chunk):
        taken = jnp.concatenate(
            [w_f32[pl.ds(e, chans, stride=chans), :] for e in range(at, at + chunk)], axis=0
        )
        w_flip[:, pl.ds(at * chans, chunk * chans)] = taken.T.astype(BF16)
    offset = column_of(b_out[...], pairs)

    each(n_all, lambda step: left_copy(step).wait())
    deep = fold * n_src * seqs
    for u in range(n_col // fold):
        taken = left_all[pl.ds(u * fold * n_src, fold * n_src)].astype(F32)
        left_flip[u] = taken.reshape(deep, rows * chans).T.astype(BF16)
    each(n_src, lambda step: right_copy(step).wait())

    factor = 1.0 / float(seqs * n_src)
    for u in range(n_col // fold):
        left = left_flip[u]
        for h in range(high):
            block = right_all[:, h].astype(F32).reshape(n_src * seqs, lanes)
            if fold == 1:
                wide = block
            else:
                lane = lax.broadcasted_iota(jnp.int32, block.shape, 1) // span
                columns = []
                for k in range(fold):
                    tall = []
                    for t in range(fold):
                        moved = block if t == k else pltpu.roll(block, ((t - k) % fold) * span, 1)
                        tall.append(jnp.where(lane == t, moved, 0.0))
                    columns.append(jnp.concatenate(tall, axis=0))
                wide = jnp.concatenate(columns, axis=1)
            product = matmul(left, wide.astype(BF16)).astype(BF16)
            for k in range(fold):
                for v in range(rows):
                    outer[
                        v // group,
                        pl.ds((h * fold + k) * chans, chans),
                        pl.ds((v % group) * lanes, lanes),
                    ] = product[v * chans : (v + 1) * chans, k * lanes : (k + 1) * lanes]
        for g in range(rows // group):
            summed = matmul(w_flip[...], outer[g])
            done = (summed * factor + offset).astype(BF16).T
            for k in range(group):
                for t in range(fold):
                    out[u * fold + t, g * group + k] = done[
                        k * lanes + t * span : k * lanes + (t + 1) * span
                    ]


def per_device(msa, scale, shift, w_left, b_left, w_right, b_right, w_out, b_out):
    seqs, span, width = msa.shape
    n_res, n_col, n_seq = lax.axis_size("res"), lax.axis_size("col"), lax.axis_size("seq")
    chans = w_left.shape[1]
    pairs = w_out.shape[1]
    n_src = n_res * n_seq
    fold = max(1, 128 // span)
    high = chans // fold
    rows = span // n_src
    lanes = fold * span
    group = max(1, 256 // lanes)
    deep = fold * n_src * seqs
    dims = (n_res, n_col, n_seq, seqs, span, width, chans, pairs)
    vmem = pl.BlockSpec(memory_space=pltpu.VMEM)
    return pl.pallas_call(
        functools.partial(kernel, dims),
        out_shape=pltpu.VMEM((n_col, rows, span, pairs), BF16),
        in_specs=[vmem] * 7 + [pl.BlockSpec(memory_space=pl.ANY), vmem],
        out_specs=vmem,
        scratch_shapes=[
            pltpu.VMEM(w_out.shape, BF16),
            pltpu.VMEM(w_out.shape, F32),
            pltpu.VMEM((pairs, chans * chans), BF16),
            pltpu.VMEM((seqs * span, 2 * chans), F32),
            pltpu.VMEM((lanes // 128, seqs * high, 128), F32),
            pltpu.VMEM((n_src, seqs, rows * chans), BF16),
            pltpu.VMEM((n_src * n_col, seqs, rows * chans), BF16),
            pltpu.VMEM((n_col // fold, rows * chans, deep), BF16),
            pltpu.VMEM((n_src, high, seqs, lanes), BF16),
            pltpu.VMEM((rows // group, chans * chans, group * lanes), BF16),
            pltpu.SemaphoreType.DMA,
            pltpu.SemaphoreType.DMA((n_src * n_col,)),
            pltpu.SemaphoreType.DMA((n_src * n_col,)),
            pltpu.SemaphoreType.DMA((n_src,)),
            pltpu.SemaphoreType.DMA((n_src,)),
        ],
        compiler_params=pltpu.CompilerParams(collective_id=0, has_side_effects=True),
    )(
        msa,
        scale.reshape(1, width),
        shift.reshape(1, width),
        w_left.T,
        b_left.reshape(1, chans),
        w_right.T,
        b_right.reshape(1, chans),
        w_out,
        b_out.reshape(1, pairs),
    )


def solution(mesh):
    return jax.shard_map(
        per_device,
        mesh=mesh,
        in_specs=(P(("groups", "res", "seq"), "col", None), P(), P(), P(), P(), P(), P(), P(), P()),
        out_specs=P("groups", ("res", "seq"), "col", None),
        check_vma=False,
    )
```

```python
import functools

import jax
import jax.numpy as jnp
from jax import lax
from jax.experimental import pallas as pl
from jax.experimental.pallas import tpu as pltpu
from jax.sharding import PartitionSpec as P

MESH = pl.DeviceIdType.MESH
F32 = jnp.float32
BF16 = jnp.bfloat16


def one_hot(shape, wanted):
    row = lax.broadcasted_iota(jnp.int32, shape, 0)
    col = lax.broadcasted_iota(jnp.int32, shape, 1)
    return jnp.where(wanted(row, col), 1.0, 0.0)


def column_of(row, size):
    spread = jnp.broadcast_to(row, (size, size))
    return jnp.sum(one_hot((size, size), lambda r, c: r == c) * spread, axis=1, keepdims=True)


def matmul(a, b):
    return jnp.dot(a, b, preferred_element_type=F32)


def matmul_turned(a, b):
    return lax.dot_general(a, b, (((1,), (1,)), ((), ())), preferred_element_type=F32)


def kernel(
    dims,
    msa,
    scale,
    shift,
    w_left,
    b_left,
    w_right,
    b_right,
    w_hbm,
    b_out,
    out,
    w_vmem,
    w_f32,
    w_flip,
    both_s,
    turn_s,
    left_send,
    left_all,
    left_flip,
    right_all,
    outer,
    w_sem,
    left_ssem,
    left_rsem,
    right_ssem,
    right_rsem,
):
    n_res, n_col, n_seq, seqs, span, width, chans, pairs = dims
    n_src = n_res * n_seq
    n_all = n_src * n_col
    fold = max(1, 128 // span)
    high = chans // fold
    rows = span // n_src
    lanes = fold * span
    group = outer.shape[2] // lanes
    res, col, seq = lax.axis_index("res"), lax.axis_index("col"), lax.axis_index("seq")
    src = res * n_seq + seq
    me = col * n_src + src

    def place(index):
        at = lax.rem(index, n_src)
        return {"res": at // n_seq, "col": index // n_src, "seq": lax.rem(at, n_seq)}

    def each(count, body):
        if count <= 16:
            for step in range(1, count):
                body(step)
        else:
            lax.fori_loop(1, count, lambda step, _: (body(step), 0)[1], 0)

    barrier = pltpu.get_barrier_semaphore()

    def greet(step):
        pl.semaphore_signal(barrier, inc=1, device_id=place(lax.rem(me + step, n_all)), device_id_type=MESH)

    each(n_all, greet)
    w_copy = pltpu.make_async_copy(w_hbm, w_vmem, w_sem)
    w_copy.start()

    w_both = jnp.concatenate([w_left[...], w_right[...]], axis=0)
    b_both = jnp.concatenate([b_left[...], b_right[...]], axis=1)
    for s in range(seqs):
        x = msa[s].astype(F32)
        mean = jnp.mean(x, axis=-1, keepdims=True)
        centred = x - mean
        variance = jnp.mean(centred * centred, axis=-1, keepdims=True)
        normed = (centred * lax.rsqrt(variance + 1e-05) * scale[...] + shift[...]).astype(BF16)
        both = matmul_turned(normed, w_both) + b_both
        both_s[pl.ds(s * span, span), :] = both
        pick = one_hot(
            (chans, 2 * chans), lambda r, c: c == chans + lax.rem(r, high) * fold + r // high
        ).astype(BF16)
        turned = matmul_turned(pick, both.astype(BF16))
        parts = [turned[k * high : (k + 1) * high] for k in range(fold)]
        whole = parts[0] if fold == 1 else jnp.concatenate(parts, axis=1)
        for k in range(lanes // 128):
            turn_s[k, pl.ds(s * high, high), :] = whole[:, k * 128 : (k + 1) * 128]

    for e in range(high):
        for k in range(lanes // 128):
            right_all[src, e, :, pl.ds(k * 128, 128)] = turn_s[
                k, pl.ds(e, seqs, stride=high), :
            ].astype(BF16)

    total = None
    for v in range(rows):
        got = jnp.concatenate(
            [both_s[pl.ds(b * rows + v, seqs, stride=span), :] for b in range(n_src)], axis=0
        )
        spot = one_hot(
            (2 * chans, rows * chans), lambda r, c: (c == v * chans + r) & (r < chans)
        ).astype(BF16)
        term = matmul(got.astype(BF16), spot)
        total = term if total is None else total + term
    total = total.reshape(n_src, seqs, rows * chans).astype(BF16)
    left_send[...] = total

    pl.semaphore_wait(barrier, n_all - 1)

    def left_copy(step):
        to = lax.rem(me + step, n_all)
        return pltpu.make_async_remote_copy(
            src_ref=left_send.at[lax.rem(to, n_src)],
            dst_ref=left_all.at[me],
            send_sem=left_ssem.at[step],
            recv_sem=left_rsem.at[step],
            device_id=place(to),
            device_id_type=MESH,
        )

    def right_copy(slot, sem, to):
        return pltpu.make_async_remote_copy(
            src_ref=right_all.at[slot],
            dst_ref=right_all.at[slot],
            send_sem=right_ssem.at[sem],
            recv_sem=right_rsem.at[sem],
            device_id=to,
            device_id_type=MESH,
        )

    def far(step):
        return right_copy(src, step, {"res": lax.rem(res + step, n_res)})

    def near(step, turn):
        slot = lax.rem(res + n_res - step, n_res) * n_seq + seq
        return right_copy(slot, turn * n_res + step, {"seq": lax.rem(seq + turn, n_seq)})

    each(n_all, lambda step: left_copy(step).start())
    each(n_res, lambda step: far(step).start())
    each(n_seq, lambda turn: near(0, turn).start())
    left_all[me] = left_send[src]

    w_copy.wait()
    w_f32[...] = w_vmem[...].astype(F32)
    chunk = 4
    for at in range(0, chans, chunk):
        taken = jnp.concatenate(
            [w_f32[pl.ds(e, chans, stride=chans), :] for e in range(at, at + chunk)], axis=0
        )
        w_flip[:, pl.ds(at * chans, chunk * chans)] = taken.T.astype(BF16)
    offset = column_of(b_out[...], pairs)

    each(n_all, lambda step: left_copy(step).wait())
    deep = fold * n_src * seqs
    for u in range(n_col // fold):
        taken = left_all[pl.ds(u * fold * n_src, fold * n_src)].astype(F32)
        left_flip[u] = taken.reshape(deep, rows * chans).T.astype(BF16)

    def relay(step):
        far(step).wait()
        each(n_seq, lambda turn: near(step, turn).start())

    each(n_res, relay)
    for step in range(n_res):
        each(n_seq, lambda turn: near(step, turn).wait())

    factor = 1.0 / float(seqs * n_src)
    for u in range(n_col // fold):
        left = left_flip[u]
        for h in range(high):
            block = right_all[:, h].astype(F32).reshape(n_src * seqs, lanes)
            if fold == 1:
                wide = block
            else:
                lane = lax.broadcasted_iota(jnp.int32, block.shape, 1) // span
                columns = []
                for k in range(fold):
                    tall = []
                    for t in range(fold):
                        moved = block if t == k else pltpu.roll(block, ((t - k) % fold) * span, 1)
                        tall.append(jnp.where(lane == t, moved, 0.0))
                    columns.append(jnp.concatenate(tall, axis=0))
                wide = jnp.concatenate(columns, axis=1)
            product = matmul(left, wide.astype(BF16)).astype(BF16)
            for k in range(fold):
                for v in range(rows):
                    outer[
                        v // group,
                        pl.ds((h * fold + k) * chans, chans),
                        pl.ds((v % group) * lanes, lanes),
                    ] = product[v * chans : (v + 1) * chans, k * lanes : (k + 1) * lanes]
        for g in range(rows // group):
            summed = matmul(w_flip[...], outer[g])
            done = (summed * factor + offset).astype(BF16).T
            for k in range(group):
                for t in range(fold):
                    out[u * fold + t, g * group + k] = done[
                        k * lanes + t * span : k * lanes + (t + 1) * span
                    ]


def per_device(msa, scale, shift, w_left, b_left, w_right, b_right, w_out, b_out):
    seqs, span, width = msa.shape
    n_res, n_col, n_seq = lax.axis_size("res"), lax.axis_size("col"), lax.axis_size("seq")
    chans = w_left.shape[1]
    pairs = w_out.shape[1]
    n_src = n_res * n_seq
    fold = max(1, 128 // span)
    high = chans // fold
    rows = span // n_src
    lanes = fold * span
    group = max(1, 256 // lanes)
    deep = fold * n_src * seqs
    dims = (n_res, n_col, n_seq, seqs, span, width, chans, pairs)
    vmem = pl.BlockSpec(memory_space=pltpu.VMEM)
    return pl.pallas_call(
        functools.partial(kernel, dims),
        out_shape=pltpu.VMEM((n_col, rows, span, pairs), BF16),
        in_specs=[vmem] * 7 + [pl.BlockSpec(memory_space=pl.ANY), vmem],
        out_specs=vmem,
        scratch_shapes=[
            pltpu.VMEM(w_out.shape, BF16),
            pltpu.VMEM(w_out.shape, F32),
            pltpu.VMEM((pairs, chans * chans), BF16),
            pltpu.VMEM((seqs * span, 2 * chans), F32),
            pltpu.VMEM((lanes // 128, seqs * high, 128), F32),
            pltpu.VMEM((n_src, seqs, rows * chans), BF16),
            pltpu.VMEM((n_src * n_col, seqs, rows * chans), BF16),
            pltpu.VMEM((n_col // fold, rows * chans, deep), BF16),
            pltpu.VMEM((n_src, high, seqs, lanes), BF16),
            pltpu.VMEM((rows // group, chans * chans, group * lanes), BF16),
            pltpu.SemaphoreType.DMA,
            pltpu.SemaphoreType.DMA((n_src * n_col,)),
            pltpu.SemaphoreType.DMA((n_src * n_col,)),
            pltpu.SemaphoreType.DMA((n_src,)),
            pltpu.SemaphoreType.DMA((n_src,)),
        ],
        compiler_params=pltpu.CompilerParams(collective_id=0, has_side_effects=True),
    )(
        msa,
        scale.reshape(1, width),
        shift.reshape(1, width),
        w_left.T,
        b_left.reshape(1, chans),
        w_right.T,
        b_right.reshape(1, chans),
        w_out,
        b_out.reshape(1, pairs),
    )


def solution(mesh):
    return jax.shard_map(
        per_device,
        mesh=mesh,
        in_specs=(P(("groups", "res", "seq"), "col", None), P(), P(), P(), P(), P(), P(), P(), P()),
        out_specs=P("groups", ("res", "seq"), "col", None),
        check_vma=False,
    )
```

```python
import functools

import jax
import jax.numpy as jnp
from jax import lax
from jax.experimental import pallas as pl
from jax.experimental.pallas import tpu as pltpu
from jax.sharding import PartitionSpec as P

MESH = pl.DeviceIdType.MESH
F32 = jnp.float32
BF16 = jnp.bfloat16


def one_hot(shape, wanted):
    row = lax.broadcasted_iota(jnp.int32, shape, 0)
    col = lax.broadcasted_iota(jnp.int32, shape, 1)
    return jnp.where(wanted(row, col), 1.0, 0.0)


def column_of(row, size):
    spread = jnp.broadcast_to(row, (size, size))
    return jnp.sum(one_hot((size, size), lambda r, c: r == c) * spread, axis=1, keepdims=True)


def matmul(a, b):
    return jnp.dot(a, b, preferred_element_type=F32)


def matmul_turned(a, b):
    return lax.dot_general(a, b, (((1,), (1,)), ((), ())), preferred_element_type=F32)


def kernel(
    dims,
    msa,
    scale,
    shift,
    w_left,
    b_left,
    w_right,
    b_right,
    w_hbm,
    b_out,
    out,
    w_vmem,
    w_f32,
    w_flip,
    both_s,
    turn_s,
    left_send,
    left_all,
    left_flip,
    right_all,
    outer,
    w_sem,
    left_ssem,
    left_rsem,
    right_ssem,
    right_rsem,
):
    n_res, n_col, n_seq, seqs, span, width, chans, pairs = dims
    n_src = n_res * n_seq
    fold = max(1, 128 // span)
    high = chans // fold
    rows = span // n_src
    lanes = fold * span
    group = outer.shape[2] // lanes
    res, col, seq = lax.axis_index("res"), lax.axis_index("col"), lax.axis_index("seq")
    src = res * n_seq + seq

    def place(at):
        return {"res": at // n_seq, "seq": lax.rem(at, n_seq)}

    def mates(step):
        if n_res & (n_res - 1):
            return lax.rem(res + step, n_res), lax.rem(res + n_res - step, n_res)
        mate, bit = 0, 1
        while bit < n_res:
            mate = mate + (res // bit + step // bit) % 2 * bit
            bit *= 2
        return mate, mate

    def each(count, body):
        if count <= 16:
            for step in range(1, count):
                body(step)
        else:
            lax.fori_loop(1, count, lambda step, _: (body(step), 0)[1], 0)

    barrier = pltpu.get_barrier_semaphore()

    def greet(to):
        pl.semaphore_signal(barrier, inc=1, device_id=to, device_id_type=MESH)

    each(n_src, lambda step: greet(place(lax.rem(src + step, n_src))))
    each(n_col, lambda turn: greet({"col": lax.rem(col + turn, n_col)}))
    w_copy = pltpu.make_async_copy(w_hbm, w_vmem, w_sem)
    w_copy.start()

    w_both = jnp.concatenate([w_left[...], w_right[...]], axis=0)
    b_both = jnp.concatenate([b_left[...], b_right[...]], axis=1)
    for s in range(seqs):
        x = msa[s].astype(F32)
        mean = jnp.mean(x, axis=-1, keepdims=True)
        centred = x - mean
        variance = jnp.mean(centred * centred, axis=-1, keepdims=True)
        normed = (centred * lax.rsqrt(variance + 1e-05) * scale[...] + shift[...]).astype(BF16)
        both = matmul_turned(normed, w_both) + b_both
        both_s[pl.ds(s * span, span), :] = both
        pick = one_hot(
            (chans, 2 * chans), lambda r, c: c == chans + lax.rem(r, high) * fold + r // high
        ).astype(BF16)
        turned = matmul_turned(pick, both.astype(BF16))
        parts = [turned[k * high : (k + 1) * high] for k in range(fold)]
        whole = parts[0] if fold == 1 else jnp.concatenate(parts, axis=1)
        for k in range(lanes // 128):
            turn_s[k, pl.ds(s * high, high), :] = whole[:, k * 128 : (k + 1) * 128]

    for e in range(high):
        for k in range(lanes // 128):
            right_all[src, e, :, pl.ds(k * 128, 128)] = turn_s[
                k, pl.ds(e, seqs, stride=high), :
            ].astype(BF16)

    total = None
    for v in range(rows):
        got = jnp.concatenate(
            [both_s[pl.ds(b * rows + v, seqs, stride=span), :] for b in range(n_src)], axis=0
        )
        spot = one_hot(
            (2 * chans, rows * chans), lambda r, c: (c == v * chans + r) & (r < chans)
        ).astype(BF16)
        term = matmul(got.astype(BF16), spot)
        total = term if total is None else total + term
    total = total.reshape(n_src, seqs, rows * chans).astype(BF16)
    left_send[...] = total

    pl.semaphore_wait(barrier, n_src + n_col - 2)

    def left_copy(step):
        to = lax.rem(src + step, n_src)
        return pltpu.make_async_remote_copy(
            src_ref=left_send.at[to],
            dst_ref=left_all.at[col, src],
            send_sem=left_ssem.at[step],
            recv_sem=left_rsem.at[step],
            device_id=place(to),
            device_id_type=MESH,
        )

    def across(turn):
        return pltpu.make_async_remote_copy(
            src_ref=left_all.at[col],
            dst_ref=left_all.at[col],
            send_sem=left_ssem.at[n_src + turn],
            recv_sem=left_rsem.at[n_src + turn],
            device_id={"col": lax.rem(col + turn, n_col)},
            device_id_type=MESH,
        )

    def right_copy(slot, sem, to):
        return pltpu.make_async_remote_copy(
            src_ref=right_all.at[slot],
            dst_ref=right_all.at[slot],
            send_sem=right_ssem.at[sem],
            recv_sem=right_rsem.at[sem],
            device_id=to,
            device_id_type=MESH,
        )

    def far(step):
        return right_copy(src, step, {"res": mates(step)[0]})

    def near(step, turn):
        slot = src if step is None else mates(step)[1] * n_seq + seq
        step = 0 if step is None else step
        return right_copy(slot, turn * n_res + step, {"seq": lax.rem(seq + turn, n_seq)})

    each(n_src, lambda step: left_copy(step).start())
    each(n_res, lambda step: far(step).start())
    each(n_seq, lambda turn: near(None, turn).start())
    left_all[col, src] = left_send[src]

    w_copy.wait()
    w_f32[...] = w_vmem[...].astype(F32)
    chunk = 4
    for at in range(0, chans, chunk):
        taken = jnp.concatenate(
            [w_f32[pl.ds(e, chans, stride=chans), :] for e in range(at, at + chunk)], axis=0
        )
        w_flip[:, pl.ds(at * chans, chunk * chans)] = taken.T.astype(BF16)
    offset = column_of(b_out[...], pairs)

    each(n_src, lambda step: left_copy(step).wait())
    each(n_col, lambda turn: across(turn).start())
    def relay(step):
        far(step).wait()
        each(n_seq, lambda turn: near(step, turn).start())

    each(n_res, relay)
    each(n_col, lambda turn: across(turn).wait())
    deep = fold * n_src * seqs
    for u in range(n_col // fold):
        taken = left_all[pl.ds(u * fold, fold)].astype(F32)
        left_flip[u] = taken.reshape(deep, rows * chans).T.astype(BF16)
    each(n_seq, lambda turn: near(None, turn).wait())
    for step in range(1, n_res):
        each(n_seq, lambda turn: near(step, turn).wait())

    factor = 1.0 / float(seqs * n_src)
    for u in range(n_col // fold):
        left = left_flip[u]
        for h in range(high):
            block = right_all[:, h].astype(F32).reshape(n_src * seqs, lanes)
            if fold == 1:
                wide = block
            else:
                lane = lax.broadcasted_iota(jnp.int32, block.shape, 1) // span
                columns = []
                for k in range(fold):
                    tall = []
                    for t in range(fold):
                        moved = block if t == k else pltpu.roll(block, ((t - k) % fold) * span, 1)
                        tall.append(jnp.where(lane == t, moved, 0.0))
                    columns.append(jnp.concatenate(tall, axis=0))
                wide = jnp.concatenate(columns, axis=1)
            product = matmul(left, wide.astype(BF16)).astype(BF16)
            for k in range(fold):
                for v in range(rows):
                    outer[
                        v // group,
                        pl.ds((h * fold + k) * chans, chans),
                        pl.ds((v % group) * lanes, lanes),
                    ] = product[v * chans : (v + 1) * chans, k * lanes : (k + 1) * lanes]
        for g in range(rows // group):
            summed = matmul(w_flip[...], outer[g])
            done = (summed * factor + offset).astype(BF16).T
            for k in range(group):
                for t in range(fold):
                    out[u * fold + t, g * group + k] = done[
                        k * lanes + t * span : k * lanes + (t + 1) * span
                    ]


def per_device(msa, scale, shift, w_left, b_left, w_right, b_right, w_out, b_out):
    seqs, span, width = msa.shape
    n_res, n_col, n_seq = lax.axis_size("res"), lax.axis_size("col"), lax.axis_size("seq")
    chans = w_left.shape[1]
    pairs = w_out.shape[1]
    n_src = n_res * n_seq
    fold = max(1, 128 // span)
    high = chans // fold
    rows = span // n_src
    lanes = fold * span
    group = max(1, 256 // lanes)
    deep = fold * n_src * seqs
    dims = (n_res, n_col, n_seq, seqs, span, width, chans, pairs)
    vmem = pl.BlockSpec(memory_space=pltpu.VMEM)
    return pl.pallas_call(
        functools.partial(kernel, dims),
        out_shape=pltpu.VMEM((n_col, rows, span, pairs), BF16),
        in_specs=[vmem] * 7 + [pl.BlockSpec(memory_space=pl.ANY), vmem],
        out_specs=vmem,
        scratch_shapes=[
            pltpu.VMEM(w_out.shape, BF16),
            pltpu.VMEM(w_out.shape, F32),
            pltpu.VMEM((pairs, chans * chans), BF16),
            pltpu.VMEM((seqs * span, 2 * chans), F32),
            pltpu.VMEM((lanes // 128, seqs * high, 128), F32),
            pltpu.VMEM((n_src, seqs, rows * chans), BF16),
            pltpu.VMEM((n_col, n_src, seqs, rows * chans), BF16),
            pltpu.VMEM((n_col // fold, rows * chans, deep), BF16),
            pltpu.VMEM((n_src, high, seqs, lanes), BF16),
            pltpu.VMEM((rows // group, chans * chans, group * lanes), BF16),
            pltpu.SemaphoreType.DMA,
            pltpu.SemaphoreType.DMA((n_src + n_col,)),
            pltpu.SemaphoreType.DMA((n_src + n_col,)),
            pltpu.SemaphoreType.DMA((n_src,)),
            pltpu.SemaphoreType.DMA((n_src,)),
        ],
        compiler_params=pltpu.CompilerParams(collective_id=0, has_side_effects=True),
    )(
        msa,
        scale.reshape(1, width),
        shift.reshape(1, width),
        w_left.T,
        b_left.reshape(1, chans),
        w_right.T,
        b_right.reshape(1, chans),
        w_out,
        b_out.reshape(1, pairs),
    )


def solution(mesh):
    return jax.shard_map(
        per_device,
        mesh=mesh,
        in_specs=(P(("groups", "res", "seq"), "col", None), P(), P(), P(), P(), P(), P(), P(), P()),
        out_specs=P("groups", ("res", "seq"), "col", None),
        check_vma=False,
    )
```

```python
import functools

import jax
import jax.numpy as jnp
from jax import lax
from jax.experimental import pallas as pl
from jax.experimental.pallas import tpu as pltpu
from jax.sharding import PartitionSpec as P

MESH = pl.DeviceIdType.MESH
F32 = jnp.float32
BF16 = jnp.bfloat16


def one_hot(shape, wanted):
    row = lax.broadcasted_iota(jnp.int32, shape, 0)
    col = lax.broadcasted_iota(jnp.int32, shape, 1)
    return jnp.where(wanted(row, col), 1.0, 0.0)


def column_of(row, size):
    spread = jnp.broadcast_to(row, (size, size))
    return jnp.sum(one_hot((size, size), lambda r, c: r == c) * spread, axis=1, keepdims=True)


def matmul(a, b):
    return jnp.dot(a, b, preferred_element_type=F32)


def matmul_turned(a, b):
    return lax.dot_general(a, b, (((1,), (1,)), ((), ())), preferred_element_type=F32)


def kernel(
    dims,
    msa,
    scale,
    shift,
    w_left,
    b_left,
    w_right,
    b_right,
    w_hbm,
    b_out,
    out,
    w_vmem,
    w_f32,
    w_flip,
    both_s,
    turn_s,
    left_send,
    left_all,
    left_flip,
    right_all,
    outer,
    w_sem,
    left_ssem,
    left_rsem,
    right_ssem,
    right_rsem,
):
    n_res, n_col, n_seq, seqs, span, width, chans, pairs = dims
    n_src = n_res * n_seq
    fold = max(1, 128 // span)
    high = chans // fold
    rows = span // n_src
    lanes = fold * span
    group = outer.shape[2] // lanes
    res, col, seq = lax.axis_index("res"), lax.axis_index("col"), lax.axis_index("seq")
    src = res * n_seq + seq

    def place(at):
        return {"res": at // n_seq, "seq": lax.rem(at, n_seq)}

    def mates(step):
        if n_res & (n_res - 1):
            return lax.rem(res + step, n_res), lax.rem(res + n_res - step, n_res)
        mate, bit = 0, 1
        while bit < n_res:
            mate = mate + (res // bit + step // bit) % 2 * bit
            bit *= 2
        return mate, mate

    def each(count, body):
        if count <= 16:
            for step in range(1, count):
                body(step)
        else:
            lax.fori_loop(1, count, lambda step, _: (body(step), 0)[1], 0)

    barrier = pltpu.get_barrier_semaphore()

    def greet(to):
        pl.semaphore_signal(barrier, inc=1, device_id=to, device_id_type=MESH)

    each(n_src, lambda step: greet(place(lax.rem(src + step, n_src))))
    each(n_col, lambda turn: greet({"col": lax.rem(col + turn, n_col)}))
    w_copy = pltpu.make_async_copy(w_hbm, w_vmem, w_sem)
    w_copy.start()

    w_both = jnp.concatenate([w_left[...], w_right[...]], axis=0)
    b_both = jnp.concatenate([b_left[...], b_right[...]], axis=1)
    for s in range(seqs):
        x = msa[s].astype(F32)
        mean = jnp.mean(x, axis=-1, keepdims=True)
        centred = x - mean
        variance = jnp.mean(centred * centred, axis=-1, keepdims=True)
        normed = (centred * lax.rsqrt(variance + 1e-05) * scale[...] + shift[...]).astype(BF16)
        both = matmul_turned(normed, w_both) + b_both
        both_s[pl.ds(s * span, span), :] = both
        pick = one_hot(
            (chans, 2 * chans), lambda r, c: c == chans + lax.rem(r, high) * fold + r // high
        ).astype(BF16)
        turned = matmul_turned(pick, both.astype(BF16))
        parts = [turned[k * high : (k + 1) * high] for k in range(fold)]
        whole = parts[0] if fold == 1 else jnp.concatenate(parts, axis=1)
        for k in range(lanes // 128):
            turn_s[k, pl.ds(s * high, high), :] = whole[:, k * 128 : (k + 1) * 128]

    for e in range(high):
        for k in range(lanes // 128):
            right_all[src, e, :, pl.ds(k * 128, 128)] = turn_s[
                k, pl.ds(e, seqs, stride=high), :
            ].astype(BF16)

    total = None
    for v in range(rows):
        got = jnp.concatenate(
            [both_s[pl.ds(b * rows + v, seqs, stride=span), :] for b in range(n_src)], axis=0
        )
        spot = one_hot(
            (2 * chans, rows * chans), lambda r, c: (c == v * chans + r) & (r < chans)
        ).astype(BF16)
        term = matmul(got.astype(BF16), spot)
        total = term if total is None else total + term
    total = total.reshape(n_src, seqs, rows * chans).astype(BF16)
    left_send[...] = total

    pl.semaphore_wait(barrier, n_src + n_col - 2)

    def left_copy(step):
        to = lax.rem(src + step, n_src)
        return pltpu.make_async_remote_copy(
            src_ref=left_send.at[to],
            dst_ref=left_all.at[col, src],
            send_sem=left_ssem.at[step],
            recv_sem=left_rsem.at[step],
            device_id=place(to),
            device_id_type=MESH,
        )

    def across(turn):
        return pltpu.make_async_remote_copy(
            src_ref=left_all.at[col],
            dst_ref=left_all.at[col],
            send_sem=left_ssem.at[n_src + turn],
            recv_sem=left_rsem.at[n_src + turn],
            device_id={"col": lax.rem(col + turn, n_col)},
            device_id_type=MESH,
        )

    def right_copy(slot, sem, to):
        return pltpu.make_async_remote_copy(
            src_ref=right_all.at[slot],
            dst_ref=right_all.at[slot],
            send_sem=right_ssem.at[sem],
            recv_sem=right_rsem.at[sem],
            device_id=to,
            device_id_type=MESH,
        )

    def far(step):
        return right_copy(src, step, {"res": mates(step)[0]})

    def near(step, turn):
        slot = src if step is None else mates(step)[1] * n_seq + seq
        step = 0 if step is None else step
        return right_copy(slot, turn * n_res + step, {"seq": lax.rem(seq + turn, n_seq)})

    each(n_src, lambda step: left_copy(step).start())
    if n_res <= 16:
        hops = {k: [abs((p ^ k) - p) for p in range(n_res)] for k in range(1, n_res)}
        for step in sorted(hops, key=lambda k: (-sum(hops[k]), -min(hops[k]))):
            far(step).start()
    else:
        each(n_res, lambda step: far(step).start())
    each(n_seq, lambda turn: near(None, turn).start())
    left_all[col, src] = left_send[src]

    w_copy.wait()
    w_f32[...] = w_vmem[...].astype(F32)
    chunk = 4
    for at in range(0, chans, chunk):
        taken = jnp.concatenate(
            [w_f32[pl.ds(e, chans, stride=chans), :] for e in range(at, at + chunk)], axis=0
        )
        w_flip[:, pl.ds(at * chans, chunk * chans)] = taken.T.astype(BF16)
    offset = column_of(b_out[...], pairs)

    each(n_src, lambda step: left_copy(step).wait())
    each(n_col, lambda turn: across(turn).start())
    def relay(step):
        far(step).wait()
        each(n_seq, lambda turn: near(step, turn).start())

    each(n_res, relay)
    each(n_col, lambda turn: across(turn).wait())
    deep = fold * n_src * seqs
    for u in range(n_col // fold):
        taken = left_all[pl.ds(u * fold, fold)].astype(F32)
        left_flip[u] = taken.reshape(deep, rows * chans).T.astype(BF16)
    each(n_seq, lambda turn: near(None, turn).wait())
    for step in range(1, n_res):
        each(n_seq, lambda turn: near(step, turn).wait())

    factor = 1.0 / float(seqs * n_src)
    for u in range(n_col // fold):
        left = left_flip[u]
        for h in range(high):
            block = right_all[:, h].astype(F32).reshape(n_src * seqs, lanes)
            if fold == 1:
                wide = block
            else:
                lane = lax.broadcasted_iota(jnp.int32, block.shape, 1) // span
                columns = []
                for k in range(fold):
                    tall = []
                    for t in range(fold):
                        moved = block if t == k else pltpu.roll(block, ((t - k) % fold) * span, 1)
                        tall.append(jnp.where(lane == t, moved, 0.0))
                    columns.append(jnp.concatenate(tall, axis=0))
                wide = jnp.concatenate(columns, axis=1)
            product = matmul(left, wide.astype(BF16)).astype(BF16)
            for k in range(fold):
                for v in range(rows):
                    outer[
                        v // group,
                        pl.ds((h * fold + k) * chans, chans),
                        pl.ds((v % group) * lanes, lanes),
                    ] = product[v * chans : (v + 1) * chans, k * lanes : (k + 1) * lanes]
        for g in range(rows // group):
            summed = matmul(w_flip[...], outer[g])
            done = (summed * factor + offset).astype(BF16).T
            for k in range(group):
                for t in range(fold):
                    out[u * fold + t, g * group + k] = done[
                        k * lanes + t * span : k * lanes + (t + 1) * span
                    ]


def per_device(msa, scale, shift, w_left, b_left, w_right, b_right, w_out, b_out):
    seqs, span, width = msa.shape
    n_res, n_col, n_seq = lax.axis_size("res"), lax.axis_size("col"), lax.axis_size("seq")
    chans = w_left.shape[1]
    pairs = w_out.shape[1]
    n_src = n_res * n_seq
    fold = max(1, 128 // span)
    high = chans // fold
    rows = span // n_src
    lanes = fold * span
    group = max(1, 256 // lanes)
    deep = fold * n_src * seqs
    dims = (n_res, n_col, n_seq, seqs, span, width, chans, pairs)
    vmem = pl.BlockSpec(memory_space=pltpu.VMEM)
    return pl.pallas_call(
        functools.partial(kernel, dims),
        out_shape=pltpu.VMEM((n_col, rows, span, pairs), BF16),
        in_specs=[vmem] * 7 + [pl.BlockSpec(memory_space=pl.ANY), vmem],
        out_specs=vmem,
        scratch_shapes=[
            pltpu.VMEM(w_out.shape, BF16),
            pltpu.VMEM(w_out.shape, F32),
            pltpu.VMEM((pairs, chans * chans), BF16),
            pltpu.VMEM((seqs * span, 2 * chans), F32),
            pltpu.VMEM((lanes // 128, seqs * high, 128), F32),
            pltpu.VMEM((n_src, seqs, rows * chans), BF16),
            pltpu.VMEM((n_col, n_src, seqs, rows * chans), BF16),
            pltpu.VMEM((n_col // fold, rows * chans, deep), BF16),
            pltpu.VMEM((n_src, high, seqs, lanes), BF16),
            pltpu.VMEM((rows // group, chans * chans, group * lanes), BF16),
            pltpu.SemaphoreType.DMA,
            pltpu.SemaphoreType.DMA((n_src + n_col,)),
            pltpu.SemaphoreType.DMA((n_src + n_col,)),
            pltpu.SemaphoreType.DMA((n_src,)),
            pltpu.SemaphoreType.DMA((n_src,)),
        ],
        compiler_params=pltpu.CompilerParams(collective_id=0, has_side_effects=True),
    )(
        msa,
        scale.reshape(1, width),
        shift.reshape(1, width),
        w_left.T,
        b_left.reshape(1, chans),
        w_right.T,
        b_right.reshape(1, chans),
        w_out,
        b_out.reshape(1, pairs),
    )


def solution(mesh):
    return jax.shard_map(
        per_device,
        mesh=mesh,
        in_specs=(P(("groups", "res", "seq"), "col", None), P(), P(), P(), P(), P(), P(), P(), P()),
        out_specs=P("groups", ("res", "seq"), "col", None),
        check_vma=False,
    )
```
